256 devices in a mesh: view: 4 (over z_lo, core), slab: 64 (over z_hi, x, y).
Axes of the slice: x: 4, y: 4, z: 8 (z_hi: 4, z_lo: 2; z = z_hi * 2 + z_lo), core: 2. Of those that a mesh axis runs over, the one named last changes fastest.
Arguments:
- atten: float32 [128, 350, 350], P('slab'), may hold values from 0.0005 to 0.008
- view_segment: int32 [8], P('view'), may hold values from 0 to 3
- efficiency: float32 [8, 488, 350], P('view'), may hold values from 0.5 to 2
- live_mask: int32 [8, 488, 350], P('view'), may hold values 0 or 1
Outputs:
- sensitivity: float32 [128, 350, 350], P('slab')
The draws below stay inside these ranges and needn't reach their ends.
All inputs are finite; a program needn't handle non-finite values. No bound on the sum of `live_mask` on one device may be relied on, other than what follows from the above.
Results may differ from the reference program's by a relative error of at most 0.0003.
Values sent between devices are 32-bit elements; how exact they have to be, the bound alone decides.
No kernel may reach another device: no remote copies, remote signals or barrier semaphores. Data moves between devices by JAX's collectives and lax.ppermute only.
A program may use at most 64 MiB of HBM per device.

```python
import math
import jax
import jax.numpy as jnp
from jax import lax

NXY = 350
NSEG = 4
VIEWS = 8
NZ = 128
NA = 488


def plant(array, own_key, least, high):
    shape = array.shape
    place = [jax.random.randint(jax.random.fold_in(own_key, axis), (), 0, shape[axis]) for axis in range(len(shape))]
    array = array.at[tuple(place)].set(least)
    longest = shape.index(max(shape))
    place[longest] = (place[longest] + 1) % shape[longest]
    return array.at[tuple(place)].set(high)


def steps_of(key, extent, shards, low, high):
    def one(position, parts):
        heights = jax.random.uniform(jax.random.fold_in(jax.random.fold_in(key, 6), position), (parts,), jnp.float32, low / len(shards), high / len(shards))
        return jnp.repeat(jnp.exp(heights), extent[position] // parts).reshape((-1,) + (1,) * (len(extent) - position - 1))

    loudness = one(*shards[0])
    for cut in shards[1:]:
        loudness = loudness * one(*cut)
    return loudness


def setup_inputs(seed: int = 0) -> dict:
    streams_of = jax.random.split(jax.random.key(seed), 5)
    return {
        "atten": jnp.clip(jnp.exp(math.log(0.008) - 2.7725887 * jax.random.uniform(streams_of[0], (NZ, NXY, NXY), jnp.float32) ** steps_of(streams_of[0], (NZ, NXY, NXY), ((0, 64),), -0.2, 0.2)), 0.0005, 0.008),
        "view_segment": plant(jax.random.randint(streams_of[1], (VIEWS,), 0, NSEG), jax.random.fold_in(streams_of[1], 1), 0, NSEG - 1).astype(jnp.int32),
        "efficiency": jnp.clip(jnp.exp(math.log(2.0) - 1.3862944 * jax.random.uniform(streams_of[2], (VIEWS, NA, NXY), jnp.float32) ** steps_of(streams_of[2], (VIEWS, NA, NXY), ((0, 4),), -0.2, 0.2)), 0.5, 2.0),
        "live_mask": plant((jax.random.randint(streams_of[3], (VIEWS, NA, NXY), 0, 10) < 9).astype(jnp.int32), jax.random.fold_in(streams_of[3], 1), 0, 1),
    }


def geometry(segment):
    angle = (45.0 + 12.0 * segment.astype(jnp.float32) / (NSEG - 1)) * (math.pi / 180.0)
    slope = jnp.cos(angle) / jnp.sin(angle)
    return (slope, jnp.sqrt(1.0 + slope * slope))

def sample_index(slope, zpos):
    rows = jnp.arange(NA).astype(jnp.float32)
    centre = rows + slope * (zpos + 0.5) - NZ - 2.0
    lower = jnp.floor(centre)
    frac = centre - lower
    lower_idx = lower.astype(jnp.int32)
    upper_idx = lower_idx + 1
    lower_ok = (lower_idx >= 0) & (lower_idx < NXY)
    upper_ok = (upper_idx >= 0) & (upper_idx < NXY)
    lower_w = jnp.where(lower_ok, 1.0 - frac, 0.0)
    upper_w = jnp.where(upper_ok, frac, 0.0)
    return (jnp.clip(lower_idx, 0, NXY - 1), lower_w, jnp.clip(upper_idx, 0, NXY - 1), upper_w)

def view_project(atten, flipped, segment):
    slope, length = geometry(segment)
    source = jnp.swapaxes(atten, 1, 2) if flipped else atten

    def one_slice(total, inputs):
        plane, zpos = inputs
        lower_idx, lower_w, upper_idx, upper_w = sample_index(slope, zpos)
        first = jnp.take(plane, lower_idx, axis=0)
        second = jnp.take(plane, upper_idx, axis=0)
        return (total + lower_w[:, None] * first + upper_w[:, None] * second, None)
    zeros = jnp.zeros((NA, NXY), jnp.float32)
    total, _ = lax.scan(one_slice, zeros, (source, jnp.arange(NZ).astype(jnp.float32)))
    return length * total

def view_back(weight, flipped, segment):
    slope, length = geometry(segment)

    def one_slice(zpos):
        lower_idx, lower_w, upper_idx, upper_w = sample_index(slope, zpos)
        plane = jnp.zeros((NXY, NXY), jnp.float32)
        plane = plane.at[lower_idx].add(lower_w[:, None] * weight)
        plane = plane.at[upper_idx].add(upper_w[:, None] * weight)
        return length * plane
    back = lax.map(one_slice, jnp.arange(NZ).astype(jnp.float32))
    return jnp.swapaxes(back, 1, 2) if flipped else back

def reference(atten, view_segment, efficiency, live_mask):
    sensitivity = jnp.zeros((NZ, NXY, NXY), jnp.float32)
    for view in range(VIEWS):
        flipped = view % 2 == 1
        ray_sum = view_project(atten, flipped, view_segment[view])
        weight = efficiency[view] * live_mask[view].astype(jnp.float32) * jnp.exp(-ray_sum)
        sensitivity = sensitivity + view_back(weight, flipped, view_segment[view])
    return sensitivity
```

```python
import math

import jax
import jax.numpy as jnp
import numpy as np
from jax import lax
from jax.experimental import pallas as pl
from jax.experimental.pallas import tpu as pltpu
from jax.sharding import Mesh
from jax.sharding import PartitionSpec as P

NSEG = 4
CELLS = 350
DEPTH = 128
RAYS = 488
LANES = 384
BINS = 12
PEERS = 16
HALF = BINS * PEERS
BLOCK = 32
ANGLE = (45.0 + 12.0 * np.arange(NSEG) / (NSEG - 1)) * (math.pi / 180.0)
SLOPE = np.cos(ANGLE) / np.sin(ANGLE)
LENGTH = np.sqrt(1.0 + SLOPE * SLOPE)
START = np.floor(
    DEPTH + 2.0 - SLOPE * (BLOCK * np.arange(DEPTH // BLOCK)[:, None] + BLOCK - 0.5)
).astype(np.int64) - 1


def pick(index, values, kind):
    result = kind(values[-1])
    for position in range(len(values) - 1):
        result = jnp.where(index == position, kind(values[position]), result)
    return result


def window_start(block, segment):
    rows = [pick(segment, START[row], jnp.int32) for row in range(DEPTH // BLOCK)]
    result = rows[-1]
    for row in range(DEPTH // BLOCK - 1):
        result = jnp.where(block == row, rows[row], result)
    return result


def geometry(block, segment):
    slope = pick(segment, SLOPE, jnp.float32)
    length = pick(segment, LENGTH, jnp.float32)
    offset = (window_start(block, segment) - (DEPTH + 2 - 64)).astype(jnp.float32)
    return slope, length, offset


def shift_of(slope, offset, place):
    centre = offset + slope * (place.astype(jnp.float32) + 0.5)
    whole = centre.astype(jnp.int32)
    return 64 - whole, centre - whole.astype(jnp.float32)


def segment_of(chunk_ref):
    return jnp.max(chunk_ref[BINS : BINS + 1, :]).astype(jnp.int32)


def arrange(place, atten_ref, out_ref, pad, flip):
    half, core = place[0], place[1]
    base = pl.multiple_of(half * HALF, 8)
    pad[...] = jnp.zeros_like(pad)
    pad[:, 0:CELLS, 0:CELLS] = atten_ref[...]

    def spread(source):
        for z in range(2):
            for peer in range(PEERS):
                skip = (BINS * peer) % 8
                rows = source[z, pl.ds(base + (BINS * peer - skip), 16), :]
                out_ref[peer, BINS * z : BINS * (z + 1), :] = rows[skip : skip + BINS]

    @pl.when(core == 1)
    def _():
        spread(pad)

    @pl.when(core == 0)
    def _():
        for z in range(2):
            for row in range(0, LANES, 128):
                for col in range(0, LANES, 128):
                    flip[z, row : row + 128, col : col + 128] = pad[
                        z, col : col + 128, row : row + 128
                    ].T
        spread(flip)


def columns(place, segment, gain_ref, live_ref, out_ref, pad):
    half, core, block, peer = place[0], place[1], place[2], place[3]
    pad[...] = jnp.zeros_like(pad)
    for view in range(2):
        pad[0:RAYS, 0:CELLS] = gain_ref[view] * live_ref[view].astype(jnp.float32)
        moved = pltpu.roll(pad[...], jnp.where(peer == 0, 0, LANES - BINS * peer), 1)
        begin = window_start(block, segment[view])
        for far in range(2):
            first = HALF * far - (HALF * far) % 128
            turned = moved[:, first : first + 128].T
            rows = turned[HALF * far - first : HALF * far - first + 16, :]
            rows = pltpu.roll(rows, 512 - begin, 1)[:, 0:LANES]
            index = lax.broadcasted_iota(jnp.int32, (16, LANES), 0)
            rows = jnp.where(index < BINS, rows, segment[view].astype(jnp.float32))
            target = 2 * jnp.bitwise_xor(half, far) + jnp.bitwise_xor(core, view)
            out_ref[target] = rows


def project(place, source_ref, c0, c1, c2, c3, out_ref):
    block = place[2]
    shapes = [geometry(block, segment_of(c)) for c in (c0, c1, c2, c3)]

    def step(peer, totals):
        totals = list(totals)
        for z in range(2):
            source = source_ref[peer, BINS * z : BINS * (z + 1), :]
            slope_x = pltpu.roll(source, LANES - 1, 1) - source
            for k in range(4):
                move, part = shift_of(shapes[k][0], shapes[k][2], BLOCK * block + 2 * peer + z)
                totals[k] = totals[k] + pltpu.roll(source + part * slope_x, move, 1)
        return tuple(totals)

    zero = jnp.zeros((BINS, LANES), jnp.float32)
    totals = lax.fori_loop(0, PEERS, step, (zero,) * 4)
    for k in range(4):
        out_ref[BINS * k : BINS * (k + 1), :] = totals[k]


def spread_back(block, shapes, weights, out_ref):
    slopes = [pltpu.roll(w, 1, 1) - w for w in weights]

    def step(peer, carry):
        for z in range(2):
            total = jnp.zeros((BINS, LANES), jnp.float32)
            for k in range(4):
                move, part = shift_of(shapes[k][0], shapes[k][2], BLOCK * block + 2 * peer + z)
                total = total + pltpu.roll(weights[k] + part * slopes[k], LANES - move, 1)
            out_ref[peer, BINS * z : BINS * (z + 1), :] = total
        return carry

    lax.fori_loop(0, PEERS, step, 0)


def weigh(place, own, below, above, across, c0, c1, c2, c3, weight_ref, out_ref):
    block = place[2]
    lane = lax.broadcasted_iota(jnp.int32, (BINS, LANES), 1)
    shapes, weights = [], []
    for k, chunk in enumerate((c0, c1, c2, c3)):
        segment = segment_of(chunk)
        shape = geometry(block, segment)
        rows = slice(BINS * k, BINS * (k + 1))
        rays = own[rows, :]
        for distance, other in ((3, below), (1, above), (2, across)):
            far = jnp.bitwise_and(block + distance, 3)
            delta = window_start(block, segment) - window_start(far, segment)
            moved = pltpu.roll(other[rows, :], jnp.where(delta > 0, LANES - delta, -delta), 1)
            inside = (lane + delta >= 0) & (lane + delta < LANES)
            rays = rays + jnp.where(inside, moved, 0.0)
        weight = shape[1] * chunk[0:BINS, :] * jnp.exp(-shape[1] * rays)
        weight_ref[rows, :] = weight
        shapes.append(shape)
        weights.append(weight)
    spread_back(block, shapes, weights, out_ref)


def spread_far(place, weight_ref, c0, c1, c2, c3, out_ref):
    block = place[2]
    shapes = [geometry(block, segment_of(c)) for c in (c2, c3, c0, c1)]
    weights = [weight_ref[BINS * k : BINS * (k + 1), :] for k in range(4)]
    spread_back(block, shapes, weights, out_ref)


def combine(place, own_near, own_far, other_near, other_far, out_ref, even, odd):
    half, core = place[0], place[1]

    def gather(target, first, second):
        for z in range(2):
            for base, source in ((0, first), (HALF, second)):
                for peer in range(PEERS):
                    row = base + BINS * peer
                    target[z, row : row + BINS, :] = source[peer, BINS * z : BINS * (z + 1), :]

    def gather_both(target, near, far):
        pl.when(half == 0)(lambda: gather(target, near, far))
        pl.when(half == 1)(lambda: gather(target, far, near))

    @pl.when(core == 0)
    def _():
        gather_both(even, own_near, own_far)
        gather_both(odd, other_near, other_far)

    @pl.when(core == 1)
    def _():
        gather_both(odd, own_near, own_far)
        gather_both(even, other_near, other_far)

    for z in range(2):
        for row in range(0, LANES, 128):
            for col in range(0, LANES, 128):
                high, wide = min(row + 128, CELLS), min(col + 128, CELLS)
                total = (
                    odd[z, row : row + 128, col : col + 128]
                    + even[z, col : col + 128, row : row + 128].T
                )
                out_ref[z, row:high, col:wide] = total[0 : high - row, 0 : wide - col]


def call(body, name, scalars, arrays, out_shapes, scratch=()):
    specs = [pl.BlockSpec(memory_space=pltpu.SMEM)] * len(scalars)
    specs += [pl.BlockSpec(memory_space=pltpu.VMEM)] * len(arrays)
    outs = [jax.ShapeDtypeStruct(shape, jnp.float32) for shape in out_shapes]
    result = pl.pallas_call(
        body,
        name=name,
        in_specs=specs,
        out_specs=[pl.BlockSpec(memory_space=pltpu.VMEM)] * len(outs),
        out_shape=outs,
        scratch_shapes=[pltpu.VMEM(shape, jnp.float32) for shape in scratch],
    )(*scalars, *arrays)
    return result


def on_device(atten, view_segment, efficiency, live_mask):
    half, core, block = lax.axis_index("zlo"), lax.axis_index("core"), lax.axis_index("zhi")
    peer = 4 * lax.axis_index("x") + lax.axis_index("y")
    place = jnp.stack([half, core, block, peer]).astype(jnp.int32)
    plane = ("x", "y")
    chunk = (PEERS, 2 * BINS, LANES)
    image = (2, LANES, LANES)

    (sent,) = call(arrange, "arrange", (place,), (atten,), [chunk], (image, image))
    source = lax.all_to_all(sent, plane, 0, 0, tiled=True)

    (gains,) = call(
        columns,
        "columns",
        (place, view_segment),
        (efficiency, live_mask),
        [(4, 16, LANES)],
        ((512, LANES),),
    )
    chunks = [gains[0]]
    for k in range(1, 4):
        pairs = [(device, device ^ k) for device in range(4)]
        chunks.append(lax.ppermute(gains[k], ("zlo", "core"), pairs))

    (rays,) = call(project, "project", (place,), (source, *chunks), [(4 * BINS, LANES)])
    others = [
        lax.ppermute(rays, "zhi", [(i, (i + d) % 4) for i in range(4)]) for d in (1, 3, 2)
    ]
    weights, near = call(
        weigh, "weigh", (place,), (rays, *others, *chunks), [(4 * BINS, LANES), chunk]
    )
    swap = [(0, 1), (1, 0)]
    near_back = lax.all_to_all(near, plane, 0, 0, tiled=True)
    far_weights = lax.ppermute(weights, "zlo", swap)
    (far,) = call(spread_far, "spread_far", (place,), (far_weights, *chunks), [chunk])
    far_back = lax.all_to_all(far, plane, 0, 0, tiled=True)
    near_other = lax.ppermute(near_back, "core", swap)
    far_other = lax.ppermute(far_back, "core", swap)
    (out,) = call(
        combine,
        "combine",
        (place,),
        (near_back, far_back, near_other, far_other),
        [(2, CELLS, CELLS)],
        (image, image),
    )
    return out


def solution(mesh):
    fine = Mesh(
        mesh.devices.reshape(2, 2, 4, 4, 4), ("zlo", "core", "zhi", "x", "y")
    )
    slab, view = ("zhi", "x", "y"), ("zlo", "core")
    return jax.shard_map(
        on_device,
        mesh=fine,
        in_specs=(P(slab, None, None), P(view), P(view, None, None), P(view, None, None)),
        out_specs=P(slab, None, None),
        check_vma=False,
    )
```

```python
import math

import jax
import jax.numpy as jnp
import numpy as np
from jax import lax
from jax.experimental import pallas as pl
from jax.experimental.pallas import tpu as pltpu
from jax.sharding import Mesh
from jax.sharding import PartitionSpec as P

NSEG = 4
CELLS = 350
DEPTH = 128
RAYS = 488
LANES = 384
PEERS = 16
TILE = 8 * PEERS
HALF = 12 * PEERS
VIEWS = 4
BLOCK = 32
ANGLE = (45.0 + 12.0 * np.arange(NSEG) / (NSEG - 1)) * (math.pi / 180.0)
SLOPE = np.cos(ANGLE) / np.sin(ANGLE)
LENGTH = np.sqrt(1.0 + SLOPE * SLOPE)
START = np.floor(
    DEPTH + 2.0 - SLOPE * (BLOCK * np.arange(DEPTH // BLOCK)[:, None] + BLOCK - 0.5)
).astype(np.int64) - 1


def pick(index, values, kind):
    result = kind(values[-1])
    for position in range(len(values) - 1):
        result = jnp.where(index == position, kind(values[position]), result)
    return result


def window_start(block, segment):
    rows = [pick(segment, START[row], jnp.int32) for row in range(DEPTH // BLOCK)]
    result = rows[-1]
    for row in range(DEPTH // BLOCK - 1):
        result = jnp.where(block == row, rows[row], result)
    return result


def geometry(block, segment):
    slope = pick(segment, SLOPE, jnp.float32)
    length = pick(segment, LENGTH, jnp.float32)
    offset = (window_start(block, segment) - (DEPTH + 2 - 64)).astype(jnp.float32)
    return slope, length, offset


def shift_of(slope, offset, place):
    centre = offset + slope * (place.astype(jnp.float32) + 0.5)
    whole = centre.astype(jnp.int32)
    return 64 - whole, centre - whole.astype(jnp.float32)


def iota(rows, lanes, axis):
    return lax.broadcasted_iota(jnp.int32, (rows, lanes), axis)


def shift_right(rows, move):
    turned = [pltpu.roll(rows[:, t : t + 128], move, 1) for t in range(0, LANES, 128)]
    low = iota(rows.shape[0], 128, 1) < move
    return jnp.concatenate([jnp.where(low, turned[t - 1], turned[t]) for t in range(3)], axis=1)


def shift_left(rows, move):
    turned = [pltpu.roll(rows[:, t : t + 128], 128 - move, 1) for t in range(0, LANES, 128)]
    low = iota(rows.shape[0], 128, 1) < 128 - move
    return jnp.concatenate(
        [jnp.where(low, turned[t], turned[(t + 1) % 3]) for t in range(3)], axis=1
    )


def halves(first, second):
    upper = iota(8, LANES, 0) < 4
    return (
        jnp.where(upper, first, pltpu.roll(second, 4, 0)),
        jnp.where(upper, pltpu.roll(first, 4, 0), second),
    )


def segments_in_order(place, chunks, segments):
    mark = (iota(8, 128, 0) == 0) & (iota(8, 128, 1) == 127)
    for k, chunk in enumerate(chunks):
        value = jnp.max(jnp.where(mark, chunk[0:8, LANES - 128 : LANES], 0.0))
        segments[jnp.bitwise_xor(2 * place[0] + place[1], k)] = value.astype(jnp.int32)


def arrange(place, atten_ref, out_ref, pad, flip):
    half, core = place[0], place[1]
    base = half * HALF
    pad[...] = jnp.zeros_like(pad)
    for z in range(2):
        pad[z, 0:CELLS, 0:CELLS] = atten_ref[:, z, :]

    def spread(source):
        for peer in range(PEERS):
            for z in range(2):
                start = pl.multiple_of(base + 8 * peer, 8)
                out_ref[peer, 8 * z : 8 * z + 8, :] = source[z, pl.ds(start, 8), :]
        for peer in range(0, PEERS, 2):
            start = pl.multiple_of(base + TILE + 4 * peer, 8)
            pair = halves(source[0, pl.ds(start, 8), :], source[1, pl.ds(start, 8), :])
            out_ref[peer, 16:24, :] = pair[0]
            out_ref[peer + 1, 16:24, :] = pair[1]

    @pl.when(core == 1)
    def _():
        spread(pad)

    @pl.when(core == 0)
    def _():
        for z in range(2):
            for row in range(0, LANES, 128):
                for col in range(0, LANES, 128):
                    flip[z, row : row + 128, col : col + 128] = pad[
                        z, col : col + 128, row : row + 128
                    ].T
        spread(flip)


def columns(place, segment, gain_ref, live_ref, same_ref, other_ref, gain, live, rows, sems):
    core, block, peer = place[1], place[2], place[3]
    copies = []
    for far in range(2):
        begin = HALF * far + 8 * peer
        rest = jnp.minimum(HALF * far + TILE + 4 * peer, CELLS - 4)
        for source, target, sem in ((gain_ref, gain, 0), (live_ref, live, 1)):
            copies.append(
                pltpu.make_async_copy(
                    source.at[pl.ds(begin, 8)], target.at[far, 0:8], sems.at[4 * far + sem]
                )
            )
            copies.append(
                pltpu.make_async_copy(
                    source.at[pl.ds(rest, 4)], target.at[far, 8:12], sems.at[4 * far + 2 + sem]
                )
            )
    for copy in copies:
        copy.start()
    skip = jnp.clip(HALF + TILE + 4 * peer - (CELLS - 4), 0, 4)
    rows[...] = jnp.zeros_like(rows)
    row = iota(8, LANES, 0)
    mark = (row == 0) & (iota(8, LANES, 1) == LANES - 1)
    for copy in copies:
        copy.wait()
    for view in range(2):
        begin = window_start(block, segment[view])
        for far in range(2):
            for low, high, at in ((0, 8, 8 * far), (8, 12, 16 + 4 * far)):
                rows[at : at + high - low, 0:RAYS] = gain[far, low:high, view, :] * live[
                    far, low:high, view, :
                ].astype(jnp.float32)
        moved = pltpu.roll(rows[...], 512 - begin, 1)[:, 0:LANES]
        first = jnp.where(mark, segment[view].astype(jnp.float32), moved[0:8])
        late = pltpu.roll(moved[16:24], jnp.where(skip == 0, 0, 8 - skip), 0)
        late = jnp.where(row < 4, moved[16:24], jnp.where(row + skip < 8, late, 0.0))

        def write(target):
            target[0:8, :] = first
            target[8:16, :] = moved[8:16]
            target[16:24, :] = late

        pl.when(core == view)(lambda: write(same_ref))
        pl.when(core != view)(lambda: write(other_ref))


def project(place, source_ref, c0, c1, c2, c3, out_ref, segments):
    block = place[2]
    segments_in_order(place, (c0, c1, c2, c3), segments)
    shapes = [geometry(block, segments[k]) for k in range(VIEWS)]
    upper = iota(8, LANES, 0) < 4

    def step(peer, totals):
        totals = list(totals)
        source = source_ref[peer]
        slope_x = shift_left(source, 1) - source
        place_z = BLOCK * block + 2 * peer
        for k in range(VIEWS):
            first, second = [shift_of(shapes[k][0], shapes[k][2], place_z + z) for z in range(2)]
            for (move, part), at in ((first, 0), (second, 8)):
                rows = source[at : at + 8] + part * slope_x[at : at + 8]
                totals[2 * k] = totals[2 * k] + shift_right(rows, move)
            rows = source[16:24] + jnp.where(upper, first[1], second[1]) * slope_x[16:24]
            rows = jnp.where(upper, shift_right(rows, first[0]), shift_right(rows, second[0]))
            totals[2 * k + 1] = totals[2 * k + 1] + rows
        return tuple(totals)

    zero = jnp.zeros((8, LANES), jnp.float32)
    totals = lax.fori_loop(0, PEERS, step, (zero,) * (2 * VIEWS), unroll=2)
    sums = [totals[2 * k] for k in range(VIEWS)]
    for k in range(0, VIEWS, 2):
        top, bottom = halves(totals[2 * k + 1], totals[2 * k + 3])
        sums.append(top + bottom)
    for position, rows in enumerate(sums):
        out_ref[8 * position : 8 * position + 8, :] = rows


def weigh(place, own, below, above, across, c0, c1, c2, c3, out_ref, segments, gains):
    half, block = place[0], place[2]
    chunks = (c0, c1, c2, c3)
    segments_in_order(place, chunks, segments)
    lane = iota(8, LANES, 1)
    upper = iota(8, LANES, 0) < 4
    for k, chunk in enumerate(chunks):
        at = jnp.bitwise_xor(2 * half + place[1], k)
        gains[at, 0:8, :] = chunk[pl.ds(pl.multiple_of(8 * half, 8), 8), :]
        gains[at, 8:16, :] = pltpu.roll(chunk[16:24, :], 4 * half, 0)
    lengths = [pick(segments[k], LENGTH, jnp.float32) for k in range(VIEWS)]
    others = [(jnp.bitwise_and(block + d, 3), ref) for d, ref in ((3, below), (1, above), (2, across))]

    def moved(rows, k, far):
        delta = window_start(block, segments[k]) - window_start(far, segments[k])
        turned = pltpu.roll(rows, jnp.where(delta > 0, LANES - delta, -delta), 1)
        return jnp.where((lane + delta >= 0) & (lane + delta < LANES), turned, 0.0)

    for k in range(VIEWS):
        rows = slice(8 * k, 8 * k + 8)
        rays = own[rows, :]
        for far, other in others:
            rays = rays + moved(other[rows, :], k, far)
        out_ref[rows, :] = lengths[k] * gains[k, 0:8, :] * jnp.exp(-lengths[k] * rays)
    for k in range(0, VIEWS, 2):
        rows = slice(32 + 4 * k, 40 + 4 * k)
        rays = own[rows, :]
        for far, other in others:
            tile = other[rows, :]
            rays = rays + jnp.where(upper, moved(tile, k, far), moved(tile, k + 1, far))
        length = jnp.where(upper, lengths[k], lengths[k + 1])
        gain = jnp.where(upper, gains[k, 8:16, :], pltpu.roll(gains[k + 1, 8:16, :], 4, 0))
        out_ref[rows, :] = length * gain * jnp.exp(-length * rays)


def spread_back(place, own, far, c0, c1, c2, c3, out_ref, segments, weights, slopes):
    half, block = place[0], place[2]
    segments_in_order(place, (c0, c1, c2, c3), segments)
    shapes = [geometry(block, segments[k]) for k in range(VIEWS)]
    for k in range(VIEWS):
        tile, rest = slice(8 * k, 8 * k + 8), slice(32 + 8 * (k // 2), 40 + 8 * (k // 2))
        pair = halves(
            jnp.where(half == 0, own[rest, :], far[rest, :]),
            jnp.where(half == 0, far[rest, :], own[rest, :]),
        )
        weights[k, 0:8, :] = jnp.where(half == 0, own[tile, :], far[tile, :])
        weights[k, 8:16, :] = jnp.where(half == 0, far[tile, :], own[tile, :])
        weights[k, 16:24, :] = pair[k % 2]
        slopes[k] = pltpu.roll(weights[k], 1, 1) - weights[k]

    def step(peer, carry):
        for z in range(2):
            total = jnp.zeros((24, LANES), jnp.float32)
            for k in range(VIEWS):
                move, part = shift_of(shapes[k][0], shapes[k][2], BLOCK * block + 2 * peer + z)
                total = total + shift_left(weights[k] + part * slopes[k], move)
            out_ref[peer, 24 * z : 24 * z + 24, :] = total
        return carry

    lax.fori_loop(0, PEERS, step, 0, unroll=2)


def combine(place, own, other, out_ref, even, odd):
    def gather(target, source):
        for z in range(2):
            for peer in range(PEERS):
                for half in range(2):
                    at = HALF * half + 8 * peer
                    rows = slice(24 * z + 8 * half, 24 * z + 8 * half + 8)
                    target[z, at : at + 8, :] = source[peer, rows, :]
            for peer in range(0, PEERS, 2):
                rows = slice(24 * z + 16, 24 * z + 24)
                pair = halves(source[peer, rows, :], source[peer + 1, rows, :])
                for half in range(2):
                    at = HALF * half + TILE + 4 * peer
                    target[z, at : at + 8, :] = pair[half]

    @pl.when(place[1] == 0)
    def _():
        gather(even, own)
        gather(odd, other)

    @pl.when(place[1] == 1)
    def _():
        gather(odd, own)
        gather(even, other)

    for z in range(2):
        for row in range(0, LANES, 128):
            for col in range(0, LANES, 128):
                high, wide = min(row + 128, CELLS), min(col + 128, CELLS)
                total = (
                    odd[z, row : row + 128, col : col + 128]
                    + even[z, col : col + 128, row : row + 128].T
                )
                out_ref[row:high, z, col:wide] = total[0 : high - row, 0 : wide - col]


def call(body, name, scalars, arrays, out_shapes, scratch=(), source=pltpu.VMEM, out=pltpu.VMEM):
    if source == pltpu.VMEM:
        arrays = [pltpu.with_memory_space_constraint(array, pltpu.VMEM) for array in arrays]
    specs = [pl.BlockSpec(memory_space=pltpu.SMEM)] * len(scalars)
    specs += [pl.BlockSpec(memory_space=source)] * len(arrays)
    if out == pltpu.VMEM:
        shapes = [pltpu.VMEM(shape, jnp.float32) for shape in out_shapes]
    else:
        shapes = [jax.ShapeDtypeStruct(shape, jnp.float32) for shape in out_shapes]
    return pl.pallas_call(
        body,
        name=name,
        in_specs=specs,
        out_specs=[pl.BlockSpec(memory_space=pltpu.VMEM)] * len(out_shapes),
        out_shape=shapes,
        scratch_shapes=scratch,
    )(*scalars, *arrays)


def on_device(atten, view_segment, efficiency, live_mask):
    half, core, block = lax.axis_index("zlo"), lax.axis_index("core"), lax.axis_index("zhi")
    peer = 4 * lax.axis_index("x") + lax.axis_index("y")
    place = jnp.stack([half, core, block, peer]).astype(jnp.int32)
    plane = ("x", "y")
    image = pltpu.VMEM((2, LANES, LANES), jnp.float32)
    views = pltpu.SMEM((VIEWS,), jnp.int32)
    rows = pltpu.VMEM((VIEWS, 24, LANES), jnp.float32)

    (sent,) = call(
        arrange,
        "arrange",
        (place,),
        (atten.transpose(1, 0, 2),),
        [(PEERS, 24, LANES)],
        (image, image),
    )
    source = lax.all_to_all(sent, plane, 0, 0, tiled=True)

    same, other = call(
        columns,
        "columns",
        (place, view_segment),
        (efficiency.transpose(2, 0, 1), live_mask.transpose(2, 0, 1)),
        [(24, LANES), (24, LANES)],
        (
            pltpu.VMEM((2, 12, 2, RAYS), jnp.float32),
            pltpu.VMEM((2, 12, 2, RAYS), jnp.int32),
            pltpu.VMEM((24, 512), jnp.float32),
            pltpu.SemaphoreType.DMA((8,)),
        ),
        source=pl.ANY,
    )
    chunks = [same]
    for k, chunk in ((1, other), (2, same), (3, other)):
        pairs = [(device, device ^ k) for device in range(4)]
        chunks.append(lax.ppermute(chunk, ("zlo", "core"), pairs))

    (rays,) = call(
        project, "project", (place,), (source, *chunks), [(12 * VIEWS, LANES)], (views,)
    )
    others = [
        lax.ppermute(rays, "zhi", [(i, (i + d) % 4) for i in range(4)]) for d in (1, 3, 2)
    ]
    (weights,) = call(
        weigh,
        "weigh",
        (place,),
        (rays, *others, *chunks),
        [(12 * VIEWS, LANES)],
        (views, pltpu.VMEM((VIEWS, 16, LANES), jnp.float32)),
    )
    swap = [(0, 1), (1, 0)]
    far = lax.ppermute(weights, "zlo", swap)
    (back,) = call(
        spread_back,
        "spread_back",
        (place,),
        (weights, far, *chunks),
        [(PEERS, 48, LANES)],
        (views, rows, rows),
    )
    back = lax.all_to_all(back, plane, 0, 0, tiled=True)
    other_back = lax.ppermute(back, "core", swap)
    (out,) = call(
        combine,
        "combine",
        (place,),
        (back, other_back),
        [(CELLS, 2, CELLS)],
        (image, image),
        out=pltpu.HBM,
    )
    return out.transpose(1, 0, 2)


def solution(mesh):
    fine = Mesh(
        mesh.devices.reshape(2, 2, 4, 4, 4), ("zlo", "core", "zhi", "x", "y")
    )
    slab, view = ("zhi", "x", "y"), ("zlo", "core")
    return jax.shard_map(
        on_device,
        mesh=fine,
        in_specs=(P(slab, None, None), P(view), P(view, None, None), P(view, None, None)),
        out_specs=P(slab, None, None),
        check_vma=False,
    )
```

```python
import math

import jax
import jax.numpy as jnp
import numpy as np
from jax import lax
from jax.experimental import pallas as pl
from jax.experimental.pallas import tpu as pltpu
from jax.sharding import Mesh
from jax.sharding import PartitionSpec as P

NSEG = 4
CELLS = 350
DEPTH = 128
RAYS = 488
LANES = 384
PEERS = 16
TILE = 8 * PEERS
HALF = 12 * PEERS
VIEWS = 4
BLOCK = 32
ANGLE = (45.0 + 12.0 * np.arange(NSEG) / (NSEG - 1)) * (math.pi / 180.0)
SLOPE = np.cos(ANGLE) / np.sin(ANGLE)
LENGTH = np.sqrt(1.0 + SLOPE * SLOPE)
START = np.floor(
    DEPTH + 2.0 - SLOPE * (BLOCK * np.arange(DEPTH // BLOCK)[:, None] + BLOCK - 0.5)
).astype(np.int64) - 1


def seat(place):
    return place[0] >> 7, (place[0] >> 6) & 1, (place[0] >> 4) & 3, place[0] & 15


def pick(index, values, kind):
    result = kind(values[-1])
    for position in range(len(values) - 1):
        result = jnp.where(index == position, kind(values[position]), result)
    return result


def window_start(block, segment):
    rows = [pick(segment, START[row], jnp.int32) for row in range(DEPTH // BLOCK)]
    result = rows[-1]
    for row in range(DEPTH // BLOCK - 1):
        result = jnp.where(block == row, rows[row], result)
    return result


def geometry(block, segment):
    slope = pick(segment, SLOPE, jnp.float32)
    length = pick(segment, LENGTH, jnp.float32)
    offset = (window_start(block, segment) - (DEPTH + 2 - 64)).astype(jnp.float32)
    return slope, length, offset


def shift_of(slope, offset, place):
    centre = offset + slope * (place.astype(jnp.float32) + 0.5)
    whole = centre.astype(jnp.int32)
    return 64 - whole, centre - whole.astype(jnp.float32)


def iota(rows, lanes, axis):
    return lax.broadcasted_iota(jnp.int32, (rows, lanes), axis)


def shift_right(rows, move):
    turned = [pltpu.roll(rows[:, t : t + 128], move, 1) for t in range(0, LANES, 128)]
    low = iota(rows.shape[0], 128, 1) < move
    return jnp.concatenate([jnp.where(low, turned[t - 1], turned[t]) for t in range(3)], axis=1)


def shift_left(rows, move):
    turned = [pltpu.roll(rows[:, t : t + 128], 128 - move, 1) for t in range(0, LANES, 128)]
    low = iota(rows.shape[0], 128, 1) < 128 - move
    return jnp.concatenate(
        [jnp.where(low, turned[t], turned[(t + 1) % 3]) for t in range(3)], axis=1
    )


def halves(first, second):
    upper = iota(8, first.shape[1], 0) < 4
    return (
        jnp.where(upper, first, pltpu.roll(second, 4, 0)),
        jnp.where(upper, pltpu.roll(first, 4, 0), second),
    )


def segments_in_order(place, chunks, segments):
    mark = (iota(8, 128, 0) == 0) & (iota(8, 128, 1) == 127)
    for k, chunk in enumerate(chunks):
        value = jnp.max(jnp.where(mark, chunk[0:8, LANES - 128 : LANES], 0.0))
        segments[jnp.bitwise_xor(place[0] >> 6, k)] = value.astype(jnp.int32)


def arrange(place, atten_ref, out_ref, rows, pad, flip, sems):
    mine = place[0] >> 6

    def fetch(low, high, sem):
        copy = pltpu.make_async_copy(
            atten_ref.at[low:high], rows.at[low:high], sems.at[sem]
        )
        copy.start()
        return copy

    def direct(half):
        base = HALF * half
        end = min(base + HALF, CELLS)
        copies = [fetch(base, base + TILE, 0), fetch(base + TILE, end, 1)]
        out_ref[:, :, LANES - 128 : LANES] = jnp.zeros((PEERS, 24, 128), jnp.float32)
        if end < base + HALF:
            rows[end : base + HALF] = jnp.zeros((base + HALF - end, 2, CELLS), jnp.float32)
        copies[0].wait()
        for peer in range(PEERS):
            at = base + 8 * peer
            for z in range(2):
                out_ref[peer, 8 * z : 8 * z + 8, 0:CELLS] = rows[at : at + 8, z, :]
        copies[1].wait()
        for peer in range(0, PEERS, 2):
            at = base + TILE + 4 * peer
            pair = halves(rows[at : at + 8, 0, :], rows[at : at + 8, 1, :])
            out_ref[peer, 16:24, 0:CELLS] = pair[0]
            out_ref[peer + 1, 16:24, 0:CELLS] = pair[1]

    def turned(half):
        cuts = [(low, min(low + 128, CELLS)) for low in range(0, CELLS, 128)]
        copies = [fetch(low, high, k) for k, (low, high) in enumerate(cuts)]
        pad[:, :, LANES - 128 : LANES] = jnp.zeros((2, LANES, 128), jnp.float32)
        pad[:, CELLS:LANES, :] = jnp.zeros((2, LANES - CELLS, LANES), jnp.float32)
        for copy, (low, high) in zip(copies, cuts):
            copy.wait()
            for z in range(2):
                pad[z, low:high, 0:CELLS] = rows[low:high, z, :]
                for col in range(0, 256, 128):
                    far = col + 128 * half
                    flip[z, col : col + 128, low : low + 128] = pad[
                        z, low : low + 128, far : far + 128
                    ].T
        base = HALF * half - 128 * half
        for peer in range(PEERS):
            at = base + 8 * peer
            for z in range(2):
                out_ref[peer, 8 * z : 8 * z + 8, :] = flip[z, at : at + 8, :]
        for peer in range(0, PEERS, 2):
            at = base + TILE + 4 * peer
            pair = halves(flip[0, at : at + 8, :], flip[1, at : at + 8, :])
            out_ref[peer, 16:24, :] = pair[0]
            out_ref[peer + 1, 16:24, :] = pair[1]

    for half in range(2):
        pl.when(mine == 2 * half)(lambda half=half: turned(half))
        pl.when(mine == 2 * half + 1)(lambda half=half: direct(half))


def columns(place, segment, gain_ref, live_ref, same_ref, other_ref, gain, live, rows, sems):
    _, core, block, peer = seat(place)
    copies = []
    for far in range(2):
        begin = HALF * far + 8 * peer
        rest = jnp.minimum(HALF * far + TILE + 4 * peer, CELLS - 4)
        for source, target, sem in ((gain_ref, gain, 0), (live_ref, live, 1)):
            copies.append(
                pltpu.make_async_copy(
                    source.at[pl.ds(begin, 8)], target.at[far, 0:8], sems.at[4 * far + sem]
                )
            )
            copies.append(
                pltpu.make_async_copy(
                    source.at[pl.ds(rest, 4)], target.at[far, 8:12], sems.at[4 * far + 2 + sem]
                )
            )
    for copy in copies:
        copy.start()
    skip = jnp.clip(HALF + TILE + 4 * peer - (CELLS - 4), 0, 4)
    rows[...] = jnp.zeros_like(rows)
    row = iota(8, LANES, 0)
    mark = (row == 0) & (iota(8, LANES, 1) == LANES - 1)
    for copy in copies:
        copy.wait()
    for view in range(2):
        begin = window_start(block, segment[view])
        for far in range(2):
            for low, high, at in ((0, 8, 8 * far), (8, 12, 16 + 4 * far)):
                rows[at : at + high - low, 0:RAYS] = gain[far, low:high, view, :] * live[
                    far, low:high, view, :
                ].astype(jnp.float32)
        moved = pltpu.roll(rows[...], 512 - begin, 1)[:, 0:LANES]
        first = jnp.where(mark, segment[view].astype(jnp.float32), moved[0:8])
        late = pltpu.roll(moved[16:24], jnp.where(skip == 0, 0, 8 - skip), 0)
        late = jnp.where(row < 4, moved[16:24], jnp.where(row + skip < 8, late, 0.0))

        def write(target):
            target[0:8, :] = first
            target[8:16, :] = moved[8:16]
            target[16:24, :] = late

        pl.when(core == view)(lambda: write(same_ref))
        pl.when(core != view)(lambda: write(other_ref))


def project(place, source_ref, c0, c1, c2, c3, out_ref, segments):
    block = seat(place)[2]
    segments_in_order(place, (c0, c1, c2, c3), segments)
    shapes = [geometry(block, segments[k]) for k in range(VIEWS)]
    upper = iota(8, LANES, 0) < 4

    def step(peer, totals):
        totals = list(totals)
        source = source_ref[peer]
        slope_x = shift_left(source, 1) - source
        place_z = BLOCK * block + 2 * peer
        for k in range(VIEWS):
            first, second = [shift_of(shapes[k][0], shapes[k][2], place_z + z) for z in range(2)]
            for (move, part), at in ((first, 0), (second, 8)):
                rows = source[at : at + 8] + part * slope_x[at : at + 8]
                totals[2 * k] = totals[2 * k] + shift_right(rows, move)
            rows = source[16:24] + jnp.where(upper, first[1], second[1]) * slope_x[16:24]
            rows = jnp.where(upper, shift_right(rows, first[0]), shift_right(rows, second[0]))
            totals[2 * k + 1] = totals[2 * k + 1] + rows
        return tuple(totals)

    zero = jnp.zeros((8, LANES), jnp.float32)
    totals = lax.fori_loop(0, PEERS, step, (zero,) * (2 * VIEWS), unroll=4)
    sums = [totals[2 * k] for k in range(VIEWS)]
    for k in range(0, VIEWS, 2):
        top, bottom = halves(totals[2 * k + 1], totals[2 * k + 3])
        sums.append(top + bottom)
    for position, rows in enumerate(sums):
        out_ref[8 * position : 8 * position + 8, :] = rows


def weigh(place, own, below, above, across, c0, c1, c2, c3, out_ref, segments, gains):
    half, _, block, _ = seat(place)
    chunks = (c0, c1, c2, c3)
    segments_in_order(place, chunks, segments)
    lane = iota(8, LANES, 1)
    upper = iota(8, LANES, 0) < 4
    for k, chunk in enumerate(chunks):
        at = jnp.bitwise_xor(place[0] >> 6, k)
        gains[at, 0:8, :] = chunk[pl.ds(pl.multiple_of(8 * half, 8), 8), :]
        gains[at, 8:16, :] = pltpu.roll(chunk[16:24, :], 4 * half, 0)
    lengths = [pick(segments[k], LENGTH, jnp.float32) for k in range(VIEWS)]
    others = [(jnp.bitwise_and(block + d, 3), ref) for d, ref in ((3, below), (1, above), (2, across))]

    def moved(rows, k, far):
        delta = window_start(block, segments[k]) - window_start(far, segments[k])
        turned = pltpu.roll(rows, jnp.where(delta > 0, LANES - delta, -delta), 1)
        return jnp.where((lane + delta >= 0) & (lane + delta < LANES), turned, 0.0)

    for k in range(VIEWS):
        rows = slice(8 * k, 8 * k + 8)
        rays = own[rows, :]
        for far, other in others:
            rays = rays + moved(other[rows, :], k, far)
        out_ref[rows, :] = lengths[k] * gains[k, 0:8, :] * jnp.exp(-lengths[k] * rays)
    for k in range(0, VIEWS, 2):
        rows = slice(32 + 4 * k, 40 + 4 * k)
        rays = own[rows, :]
        for far, other in others:
            tile = other[rows, :]
            rays = rays + jnp.where(upper, moved(tile, k, far), moved(tile, k + 1, far))
        length = jnp.where(upper, lengths[k], lengths[k + 1])
        gain = jnp.where(upper, gains[k, 8:16, :], pltpu.roll(gains[k + 1, 8:16, :], 4, 0))
        out_ref[rows, :] = length * gain * jnp.exp(-length * rays)


def spread_back(place, own, far, c0, c1, c2, c3, out_ref, segments, weights, slopes):
    half, _, block, _ = seat(place)
    segments_in_order(place, (c0, c1, c2, c3), segments)
    shapes = [geometry(block, segments[k]) for k in range(VIEWS)]
    for k in range(VIEWS):
        tile, rest = slice(8 * k, 8 * k + 8), slice(32 + 8 * (k // 2), 40 + 8 * (k // 2))
        pair = halves(
            jnp.where(half == 0, own[rest, :], far[rest, :]),
            jnp.where(half == 0, far[rest, :], own[rest, :]),
        )
        weights[k, 0:8, :] = jnp.where(half == 0, own[tile, :], far[tile, :])
        weights[k, 8:16, :] = jnp.where(half == 0, far[tile, :], own[tile, :])
        weights[k, 16:24, :] = pair[k % 2]
        slopes[k] = pltpu.roll(weights[k], 1, 1) - weights[k]

    def step(peer, carry):
        for z in range(2):
            total = jnp.zeros((24, LANES), jnp.float32)
            for k in range(VIEWS):
                move, part = shift_of(shapes[k][0], shapes[k][2], BLOCK * block + 2 * peer + z)
                total = total + shift_left(weights[k] + part * slopes[k], move)
            out_ref[peer, 24 * z : 24 * z + 24, :] = total
        return carry

    lax.fori_loop(0, PEERS, step, 0, unroll=4)


def combine(place, own, other, out_ref, even, odd, image, sems):
    core = seat(place)[1]

    def gather(target, source):
        for z in range(2):
            for peer in range(PEERS):
                for half in range(2):
                    at = HALF * half + 8 * peer
                    rows = slice(24 * z + 8 * half, 24 * z + 8 * half + 8)
                    target[z, at : at + 8, :] = source[peer, rows, :]
            for peer in range(0, PEERS, 2):
                rows = slice(24 * z + 16, 24 * z + 24)
                pair = halves(source[peer, rows, :], source[peer + 1, rows, :])
                for half in range(2):
                    at = HALF * half + TILE + 4 * peer
                    target[z, at : at + 8, :] = pair[half]

    @pl.when(core == 0)
    def _():
        gather(even, own)
        gather(odd, other)

    @pl.when(core == 1)
    def _():
        gather(odd, own)
        gather(even, other)

    copies = []
    for row in range(0, LANES, 128):
        high = min(row + 128, CELLS)
        for z in range(2):
            for col in range(0, LANES, 128):
                wide = min(col + 128, CELLS)
                total = (
                    odd[z, row : row + 128, col : col + 128]
                    + even[z, col : col + 128, row : row + 128].T
                )
                image[row:high, z, col:wide] = total[0 : high - row, 0 : wide - col]
        copy = pltpu.make_async_copy(
            image.at[row:high], out_ref.at[row:high], sems.at[len(copies)]
        )
        copy.start()
        copies.append(copy)
    for copy in copies:
        copy.wait()


def call(body, name, scalars, arrays, out_shapes, scratch=(), source=pltpu.VMEM, out=pltpu.VMEM):
    if source == pltpu.VMEM:
        arrays = [pltpu.with_memory_space_constraint(array, pltpu.VMEM) for array in arrays]
    specs = [pl.BlockSpec(memory_space=pltpu.SMEM)] * len(scalars)
    specs += [pl.BlockSpec(memory_space=source)] * len(arrays)
    if out == pltpu.VMEM:
        shapes = [pltpu.VMEM(shape, jnp.float32) for shape in out_shapes]
    else:
        shapes = [jax.ShapeDtypeStruct(shape, jnp.float32) for shape in out_shapes]
    return pl.pallas_call(
        body,
        name=name,
        in_specs=specs,
        out_specs=[pl.BlockSpec(memory_space=out)] * len(out_shapes),
        out_shape=shapes,
        scratch_shapes=scratch,
    )(*scalars, *arrays)


def on_device(atten, view_segment, efficiency, live_mask):
    place = lax.axis_index(("zlo", "core", "zhi", "x", "y")).reshape(1)
    plane = ("x", "y")
    image = pltpu.VMEM((2, LANES, LANES), jnp.float32)
    views = pltpu.SMEM((VIEWS,), jnp.int32)
    rows = pltpu.VMEM((VIEWS, 24, LANES), jnp.float32)

    (sent,) = call(
        arrange,
        "arrange",
        (place,),
        (atten.transpose(1, 0, 2),),
        [(PEERS, 24, LANES)],
        (
            pltpu.VMEM((LANES, 2, CELLS), jnp.float32),
            image,
            pltpu.VMEM((2, 256, LANES), jnp.float32),
            pltpu.SemaphoreType.DMA((3,)),
        ),
        source=pl.ANY,
    )
    source = lax.all_to_all(sent, plane, 0, 0, tiled=True)

    same, other = call(
        columns,
        "columns",
        (place, view_segment),
        (efficiency.transpose(2, 0, 1), live_mask.transpose(2, 0, 1)),
        [(24, LANES), (24, LANES)],
        (
            pltpu.VMEM((2, 12, 2, RAYS), jnp.float32),
            pltpu.VMEM((2, 12, 2, RAYS), jnp.int32),
            pltpu.VMEM((24, 512), jnp.float32),
            pltpu.SemaphoreType.DMA((8,)),
        ),
        source=pl.ANY,
    )
    chunks = [same]
    for k, chunk in ((1, other), (2, same), (3, other)):
        pairs = [(device, device ^ k) for device in range(4)]
        chunks.append(lax.ppermute(chunk, ("zlo", "core"), pairs))

    (rays,) = call(
        project, "project", (place,), (source, *chunks), [(12 * VIEWS, LANES)], (views,)
    )
    others = [
        lax.ppermute(rays, "zhi", [(i, (i + d) % 4) for i in range(4)]) for d in (1, 3, 2)
    ]
    (weights,) = call(
        weigh,
        "weigh",
        (place,),
        (rays, *others, *chunks),
        [(12 * VIEWS, LANES)],
        (views, pltpu.VMEM((VIEWS, 16, LANES), jnp.float32)),
    )
    swap = [(0, 1), (1, 0)]
    far = lax.ppermute(weights, "zlo", swap)
    (back,) = call(
        spread_back,
        "spread_back",
        (place,),
        (weights, far, *chunks),
        [(PEERS, 48, LANES)],
        (views, rows, rows),
    )
    back = lax.all_to_all(back, plane, 0, 0, tiled=True)
    other_back = lax.ppermute(back, "core", swap)
    (out,) = call(
        combine,
        "combine",
        (place,),
        (back, other_back),
        [(CELLS, 2, CELLS)],
        (
            image,
            image,
            pltpu.VMEM((CELLS, 2, CELLS), jnp.float32),
            pltpu.SemaphoreType.DMA((3,)),
        ),
        out=pl.ANY,
    )
    return out.transpose(1, 0, 2)


def solution(mesh):
    fine = Mesh(
        mesh.devices.reshape(2, 2, 4, 4, 4), ("zlo", "core", "zhi", "x", "y")
    )
    slab, view = ("zhi", "x", "y"), ("zlo", "core")
    return jax.shard_map(
        on_device,
        mesh=fine,
        in_specs=(P(slab, None, None), P(view), P(view, None, None), P(view, None, None)),
        out_specs=P(slab, None, None),
        check_vma=False,
    )
```

```python
import math

import jax
import jax.numpy as jnp
import numpy as np
from jax import lax
from jax.experimental import pallas as pl
from jax.experimental.pallas import tpu as pltpu
from jax.sharding import Mesh
from jax.sharding import PartitionSpec as P

NSEG = 4
CELLS = 350
DEPTH = 128
RAYS = 488
LANES = 384
PEERS = 16
TILE = 8 * PEERS
HALF = 12 * PEERS
VIEWS = 4
BLOCK = 32
ANGLE = (45.0 + 12.0 * np.arange(NSEG) / (NSEG - 1)) * (math.pi / 180.0)
SLOPE = np.cos(ANGLE) / np.sin(ANGLE)
LENGTH = np.sqrt(1.0 + SLOPE * SLOPE)
START = np.floor(
    DEPTH + 2.0 - SLOPE * (BLOCK * np.arange(DEPTH // BLOCK)[:, None] + BLOCK - 0.5)
).astype(np.int64) - 1


def seat(place):
    return place[0] >> 7, (place[0] >> 6) & 1, (place[0] >> 4) & 3, place[0] & 15


def pick(index, values, kind):
    result = kind(values[-1])
    for position in range(len(values) - 1):
        result = jnp.where(index == position, kind(values[position]), result)
    return result


def window_start(block, segment):
    rows = [pick(segment, START[row], jnp.int32) for row in range(DEPTH // BLOCK)]
    result = rows[-1]
    for row in range(DEPTH // BLOCK - 1):
        result = jnp.where(block == row, rows[row], result)
    return result


def geometry(block, segment):
    slope = pick(segment, SLOPE, jnp.float32)
    length = pick(segment, LENGTH, jnp.float32)
    offset = (window_start(block, segment) - (DEPTH + 2 - 64)).astype(jnp.float32)
    return slope, length, offset


def shift_of(slope, offset, place):
    centre = offset + slope * (place.astype(jnp.float32) + 0.5)
    whole = centre.astype(jnp.int32)
    return 64 - whole, centre - whole.astype(jnp.float32)


def iota(rows, lanes, axis):
    return lax.broadcasted_iota(jnp.int32, (rows, lanes), axis)


def shift_right(rows, move):
    turned = [pltpu.roll(rows[:, t : t + 128], move, 1) for t in range(0, LANES, 128)]
    low = iota(rows.shape[0], 128, 1) < move
    return jnp.concatenate([jnp.where(low, turned[t - 1], turned[t]) for t in range(3)], axis=1)


def shift_left(rows, move):
    turned = [pltpu.roll(rows[:, t : t + 128], 128 - move, 1) for t in range(0, LANES, 128)]
    low = iota(rows.shape[0], 128, 1) < 128 - move
    return jnp.concatenate(
        [jnp.where(low, turned[t], turned[(t + 1) % 3]) for t in range(3)], axis=1
    )


def halves(first, second):
    upper = iota(8, first.shape[1], 0) < 4
    return (
        jnp.where(upper, first, pltpu.roll(second, 4, 0)),
        jnp.where(upper, pltpu.roll(first, 4, 0), second),
    )


def segments_in_order(place, chunks, segments):
    mark = (iota(8, 128, 0) == 0) & (iota(8, 128, 1) == 127)
    for k, chunk in enumerate(chunks):
        value = jnp.max(jnp.where(mark, chunk[0:8, LANES - 128 : LANES], 0.0))
        segments[jnp.bitwise_xor(place[0] >> 6, k)] = value.astype(jnp.int32)


def arrange(place, atten_ref, out_ref, rows, pad, flip, sems):
    mine = place[0] >> 6

    def fetch(low, high, sem):
        copy = pltpu.make_async_copy(
            atten_ref.at[low:high], rows.at[low:high], sems.at[sem]
        )
        copy.start()
        return copy

    def direct(half):
        base = HALF * half
        end = min(base + HALF, CELLS)
        copies = [fetch(base, base + TILE, 0), fetch(base + TILE, end, 1)]
        out_ref[:, :, LANES - 128 : LANES] = jnp.zeros((PEERS, 24, 128), jnp.float32)
        if end < base + HALF:
            rows[end : base + HALF] = jnp.zeros((base + HALF - end, 2, CELLS), jnp.float32)
        copies[0].wait()
        for peer in range(PEERS):
            at = base + 8 * peer
            for z in range(2):
                out_ref[peer, 8 * z : 8 * z + 8, 0:CELLS] = rows[at : at + 8, z, :]
        copies[1].wait()
        for peer in range(0, PEERS, 2):
            at = base + TILE + 4 * peer
            pair = halves(rows[at : at + 8, 0, :], rows[at : at + 8, 1, :])
            out_ref[peer, 16:24, 0:CELLS] = pair[0]
            out_ref[peer + 1, 16:24, 0:CELLS] = pair[1]

    def turned(half):
        cuts = [(low, min(low + 128, CELLS)) for low in range(0, CELLS, 128)]
        copies = [fetch(low, high, k) for k, (low, high) in enumerate(cuts)]
        pad[:, :, LANES - 128 : LANES] = jnp.zeros((2, LANES, 128), jnp.float32)
        pad[:, CELLS:LANES, :] = jnp.zeros((2, LANES - CELLS, LANES), jnp.float32)
        for copy, (low, high) in zip(copies, cuts):
            copy.wait()
            for z in range(2):
                pad[z, low:high, 0:CELLS] = rows[low:high, z, :]
                for col in range(0, 256, 128):
                    far = col + 128 * half
                    flip[z, col : col + 128, low : low + 128] = pad[
                        z, low : low + 128, far : far + 128
                    ].T
        base = HALF * half - 128 * half
        for peer in range(PEERS):
            at = base + 8 * peer
            for z in range(2):
                out_ref[peer, 8 * z : 8 * z + 8, :] = flip[z, at : at + 8, :]
        for peer in range(0, PEERS, 2):
            at = base + TILE + 4 * peer
            pair = halves(flip[0, at : at + 8, :], flip[1, at : at + 8, :])
            out_ref[peer, 16:24, :] = pair[0]
            out_ref[peer + 1, 16:24, :] = pair[1]

    for half in range(2):
        pl.when(mine == 2 * half)(lambda half=half: turned(half))
        pl.when(mine == 2 * half + 1)(lambda half=half: direct(half))


def columns(place, segment, gain_ref, live_ref, same_ref, other_ref, gain, live, rows, sems):
    _, core, block, peer = seat(place)
    copies = []
    for far in range(2):
        begin = HALF * far + 8 * peer
        rest = jnp.minimum(HALF * far + TILE + 4 * peer, CELLS - 4)
        for source, target, sem in ((gain_ref, gain, 0), (live_ref, live, 1)):
            copies.append(
                pltpu.make_async_copy(
                    source.at[pl.ds(begin, 8)], target.at[far, 0:8], sems.at[4 * far + sem]
                )
            )
            copies.append(
                pltpu.make_async_copy(
                    source.at[pl.ds(rest, 4)], target.at[far, 8:12], sems.at[4 * far + 2 + sem]
                )
            )
    for copy in copies:
        copy.start()
    skip = jnp.clip(HALF + TILE + 4 * peer - (CELLS - 4), 0, 4)
    rows[...] = jnp.zeros_like(rows)
    row = iota(8, LANES, 0)
    mark = (row == 0) & (iota(8, LANES, 1) == LANES - 1)
    for copy in copies:
        copy.wait()
    for view in range(2):
        begin = window_start(block, segment[view])
        for far in range(2):
            for low, high, at in ((0, 8, 8 * far), (8, 12, 16 + 4 * far)):
                rows[at : at + high - low, 0:RAYS] = gain[far, low:high, view, :] * live[
                    far, low:high, view, :
                ].astype(jnp.float32)
        moved = pltpu.roll(rows[...], 512 - begin, 1)[:, 0:LANES]
        first = jnp.where(mark, segment[view].astype(jnp.float32), moved[0:8])
        late = pltpu.roll(moved[16:24], jnp.where(skip == 0, 0, 8 - skip), 0)
        late = jnp.where(row < 4, moved[16:24], jnp.where(row + skip < 8, late, 0.0))

        def write(target):
            target[0:8, :] = first
            target[8:16, :] = moved[8:16]
            target[16:24, :] = late

        pl.when(core == view)(lambda: write(same_ref))
        pl.when(core != view)(lambda: write(other_ref))


def project(place, source_ref, c0, c1, c2, c3, out_ref, segments):
    block = seat(place)[2]
    segments_in_order(place, (c0, c1, c2, c3), segments)
    shapes = [geometry(block, segments[k]) for k in range(VIEWS)]
    upper = iota(8, LANES, 0) < 4

    def step(peer, totals):
        totals = list(totals)
        source = source_ref[peer]
        slope_x = shift_left(source, 1) - source
        place_z = BLOCK * block + 2 * peer
        for k in range(VIEWS):
            first, second = [shift_of(shapes[k][0], shapes[k][2], place_z + z) for z in range(2)]
            for (move, part), at in ((first, 0), (second, 8)):
                rows = source[at : at + 8] + part * slope_x[at : at + 8]
                totals[2 * k] = totals[2 * k] + shift_right(rows, move)
            rows = source[16:24] + jnp.where(upper, first[1], second[1]) * slope_x[16:24]
            rows = jnp.where(upper, shift_right(rows, first[0]), shift_right(rows, second[0]))
            totals[2 * k + 1] = totals[2 * k + 1] + rows
        return tuple(totals)

    zero = jnp.zeros((8, LANES), jnp.float32)
    totals = lax.fori_loop(0, PEERS, step, (zero,) * (2 * VIEWS), unroll=16)
    sums = [totals[2 * k] for k in range(VIEWS)]
    for k in range(0, VIEWS, 2):
        top, bottom = halves(totals[2 * k + 1], totals[2 * k + 3])
        sums.append(top + bottom)
    for position, rows in enumerate(sums):
        out_ref[8 * position : 8 * position + 8, :] = rows


def weigh(place, own, below, above, across, c0, c1, c2, c3, out_ref, segments, gains):
    half, _, block, _ = seat(place)
    chunks = (c0, c1, c2, c3)
    segments_in_order(place, chunks, segments)
    lane = iota(8, LANES, 1)
    upper = iota(8, LANES, 0) < 4
    for k, chunk in enumerate(chunks):
        at = jnp.bitwise_xor(place[0] >> 6, k)
        gains[at, 0:8, :] = chunk[pl.ds(pl.multiple_of(8 * half, 8), 8), :]
        gains[at, 8:16, :] = pltpu.roll(chunk[16:24, :], 4 * half, 0)
    lengths = [pick(segments[k], LENGTH, jnp.float32) for k in range(VIEWS)]
    others = [(jnp.bitwise_and(block + d, 3), ref) for d, ref in ((3, below), (1, above), (2, across))]

    def moved(rows, k, far):
        delta = window_start(block, segments[k]) - window_start(far, segments[k])
        turned = pltpu.roll(rows, jnp.where(delta > 0, LANES - delta, -delta), 1)
        return jnp.where((lane + delta >= 0) & (lane + delta < LANES), turned, 0.0)

    for k in range(VIEWS):
        rows = slice(8 * k, 8 * k + 8)
        rays = own[rows, :]
        for far, other in others:
            rays = rays + moved(other[rows, :], k, far)
        out_ref[rows, :] = lengths[k] * gains[k, 0:8, :] * jnp.exp(-lengths[k] * rays)
    for k in range(0, VIEWS, 2):
        rows = slice(32 + 4 * k, 40 + 4 * k)
        rays = own[rows, :]
        for far, other in others:
            tile = other[rows, :]
            rays = rays + jnp.where(upper, moved(tile, k, far), moved(tile, k + 1, far))
        length = jnp.where(upper, lengths[k], lengths[k + 1])
        gain = jnp.where(upper, gains[k, 8:16, :], pltpu.roll(gains[k + 1, 8:16, :], 4, 0))
        out_ref[rows, :] = length * gain * jnp.exp(-length * rays)


def spread_back(place, own, far, c0, c1, c2, c3, out_ref, segments, weights, slopes):
    half, _, block, _ = seat(place)
    segments_in_order(place, (c0, c1, c2, c3), segments)
    shapes = [geometry(block, segments[k]) for k in range(VIEWS)]
    for k in range(VIEWS):
        tile, rest = slice(8 * k, 8 * k + 8), slice(32 + 8 * (k // 2), 40 + 8 * (k // 2))
        pair = halves(
            jnp.where(half == 0, own[rest, :], far[rest, :]),
            jnp.where(half == 0, far[rest, :], own[rest, :]),
        )
        weights[k, 0:8, :] = jnp.where(half == 0, own[tile, :], far[tile, :])
        weights[k, 8:16, :] = jnp.where(half == 0, far[tile, :], own[tile, :])
        weights[k, 16:24, :] = pair[k % 2]
        slopes[k] = pltpu.roll(weights[k], 1, 1) - weights[k]

    def step(peer, carry):
        for z in range(2):
            total = jnp.zeros((24, LANES), jnp.float32)
            for k in range(VIEWS):
                move, part = shift_of(shapes[k][0], shapes[k][2], BLOCK * block + 2 * peer + z)
                total = total + shift_left(weights[k] + part * slopes[k], move)
            out_ref[peer, 24 * z : 24 * z + 24, :] = total
        return carry

    lax.fori_loop(0, PEERS, step, 0, unroll=16)


def combine(place, own, other, out_ref, even, odd, image, sems):
    core = seat(place)[1]

    def gather(target, source):
        for z in range(2):
            for peer in range(PEERS):
                for half in range(2):
                    at = HALF * half + 8 * peer
                    rows = slice(24 * z + 8 * half, 24 * z + 8 * half + 8)
                    target[z, at : at + 8, :] = source[peer, rows, :]
            for peer in range(0, PEERS, 2):
                rows = slice(24 * z + 16, 24 * z + 24)
                pair = halves(source[peer, rows, :], source[peer + 1, rows, :])
                for half in range(2):
                    at = HALF * half + TILE + 4 * peer
                    target[z, at : at + 8, :] = pair[half]

    @pl.when(core == 0)
    def _():
        gather(even, own)
        gather(odd, other)

    @pl.when(core == 1)
    def _():
        gather(odd, own)
        gather(even, other)

    copies = []
    for row in range(0, LANES, 128):
        high = min(row + 128, CELLS)
        for z in range(2):
            for col in range(0, LANES, 128):
                wide = min(col + 128, CELLS)
                total = (
                    odd[z, row : row + 128, col : col + 128]
                    + even[z, col : col + 128, row : row + 128].T
                )
                image[row:high, z, col:wide] = total[0 : high - row, 0 : wide - col]
        copy = pltpu.make_async_copy(
            image.at[row:high], out_ref.at[row:high], sems.at[len(copies)]
        )
        copy.start()
        copies.append(copy)
    for copy in copies:
        copy.wait()


def call(body, scalars, arrays, out_shapes, scratch=(), source=pltpu.VMEM, out=pltpu.VMEM):
    if source == pltpu.VMEM:
        arrays = [pltpu.with_memory_space_constraint(array, pltpu.VMEM) for array in arrays]
    specs = [pl.BlockSpec(memory_space=pltpu.SMEM)] * len(scalars)
    specs += [pl.BlockSpec(memory_space=source)] * len(arrays)
    if out == pltpu.VMEM:
        shapes = [pltpu.VMEM(shape, jnp.float32) for shape in out_shapes]
    else:
        shapes = [jax.ShapeDtypeStruct(shape, jnp.float32) for shape in out_shapes]
    return pl.pallas_call(
        body,
        in_specs=specs,
        out_specs=[pl.BlockSpec(memory_space=out)] * len(out_shapes),
        out_shape=shapes,
        scratch_shapes=scratch,
    )(*scalars, *arrays)


def on_device(atten, view_segment, efficiency, live_mask):
    place = lax.axis_index(("zlo", "core", "zhi", "x", "y")).reshape(1)
    plane = ("x", "y")
    image = pltpu.VMEM((2, LANES, LANES), jnp.float32)
    views = pltpu.SMEM((VIEWS,), jnp.int32)
    rows = pltpu.VMEM((VIEWS, 24, LANES), jnp.float32)

    (sent,) = call(
        arrange,
        (place,),
        (atten.transpose(1, 0, 2),),
        [(PEERS, 24, LANES)],
        (
            pltpu.VMEM((LANES, 2, CELLS), jnp.float32),
            image,
            pltpu.VMEM((2, 256, LANES), jnp.float32),
            pltpu.SemaphoreType.DMA((3,)),
        ),
        source=pl.ANY,
    )
    source = lax.all_to_all(sent, plane, 0, 0, tiled=True)

    same, other = call(
        columns,
        (place, view_segment),
        (efficiency.transpose(2, 0, 1), live_mask.transpose(2, 0, 1)),
        [(24, LANES), (24, LANES)],
        (
            pltpu.VMEM((2, 12, 2, RAYS), jnp.float32),
            pltpu.VMEM((2, 12, 2, RAYS), jnp.int32),
            pltpu.VMEM((24, 512), jnp.float32),
            pltpu.SemaphoreType.DMA((8,)),
        ),
        source=pl.ANY,
    )
    chunks = [same]
    for k, chunk in ((1, other), (2, same), (3, other)):
        pairs = [(device, device ^ k) for device in range(4)]
        chunks.append(lax.ppermute(chunk, ("zlo", "core"), pairs))

    (rays,) = call(project, (place,), (source, *chunks), [(12 * VIEWS, LANES)], (views,))
    others = []
    for distance in (1, 3, 2):
        pairs = [(i, (i + distance) % 4) for i in range(4)]
        others.append(lax.ppermute(rays, "zhi", pairs))
    (weights,) = call(
        weigh,
        (place,),
        (rays, *others, *chunks),
        [(12 * VIEWS, LANES)],
        (views, pltpu.VMEM((VIEWS, 16, LANES), jnp.float32)),
    )
    swap = [(0, 1), (1, 0)]
    far = lax.ppermute(weights, "zlo", swap)
    (back,) = call(
        spread_back, (place,), (weights, far, *chunks), [(PEERS, 48, LANES)], (views, rows, rows)
    )
    back = lax.all_to_all(back, plane, 0, 0, tiled=True)
    other_back = lax.ppermute(back, "core", swap)
    (out,) = call(
        combine,
        (place,),
        (back, other_back),
        [(CELLS, 2, CELLS)],
        (
            image,
            image,
            pltpu.VMEM((CELLS, 2, CELLS), jnp.float32),
            pltpu.SemaphoreType.DMA((3,)),
        ),
        out=pl.ANY,
    )
    return out.transpose(1, 0, 2)


def solution(mesh):
    fine = Mesh(
        mesh.devices.reshape(2, 2, 4, 4, 4), ("zlo", "core", "zhi", "x", "y")
    )
    slab, view = ("zhi", "x", "y"), ("zlo", "core")
    return jax.shard_map(
        on_device,
        mesh=fine,
        in_specs=(P(slab, None, None), P(view), P(view, None, None), P(view, None, None)),
        out_specs=P(slab, None, None),
        check_vma=False,
    )
```
